32 devices in a mesh: fsdp: 8 (over y, x, core), rep: 4 (over z).
Axes of the slice: x: 2, y: 2, z: 4, core: 2. Of those that a mesh axis runs over, the one named last changes fastest.
Arguments:
- inputs: bfloat16 [4, 1024, 4096], P('rep', 'fsdp'), may hold values from -6 to 6
- out_grad: bfloat16 [4, 1024, 512], P('rep', 'fsdp'), may hold values from -6 to 6
- weight: bfloat16 [4096, 512], P('fsdp'), may hold values from -6 to 6
- momentum: float32 [4, 512, 4096], P('rep', 'fsdp'), may hold values from -6 to 6
- band_index: int32 [128], replicated, may hold values from 0 to 511, as said below
Outputs:
- leftover: float32 [4, 512, 4096], P('rep', 'fsdp')
- new_weight: bfloat16 [4096, 512], P('fsdp')
- values: bfloat16 [4, 1024, 512], P('rep', 'fsdp')
The draws below stay inside these ranges and needn't reach their ends.
Inputs may be any that keep to these rules, and one draw needn't show every extreme that they name: `band_index`: distinct entries below 512; 0 and 511 are always among them.
All inputs are finite; a program needn't handle non-finite values.
Results may differ from the reference program's by a relative error of at most 0.0049.
Values may be sent and summed in bfloat16 or wider, within the bound.
A program may use at most 64 MiB of HBM per device.

```python
import math
import jax
import jax.numpy as jnp
from jax import lax

D = 4096
KVW = 512
GROUP = 4096
BAND = 128
LOW = 512
TOKENS = 1024
GROUPS = 512
N_REP = 4


def draw_band_index(key, part):
    middle = jax.random.permutation(jax.random.fold_in(key, 7), LOW - 2)[:BAND - 2] + 1
    ends = jnp.array([0, LOW - 1], dtype=jnp.int32)
    return jnp.concatenate([ends, middle.astype(jnp.int32)]).astype(jnp.int32)


def spiked(entries, rng, source, target, blocks, factor):
    def block_of(axis_at):
        return (jnp.arange(entries.shape[axis_at]) // (entries.shape[axis_at] // blocks)).reshape((-1,) + (1,) * (entries.ndim - 1 - axis_at))

    first = jax.random.permutation(rng, blocks)[block_of(target)]
    second = (block_of(target) + blocks // 2) % blocks
    return jnp.where((block_of(source) == first) | (block_of(source) == second), factor * entries, entries)


def shard_levels(own_key, dims, cuts, low, largest):
    loudness = 1.0
    for axis_at, parts in cuts:
        heights = jax.random.uniform(jax.random.fold_in(jax.random.fold_in(own_key, 6), axis_at), (parts,), jnp.float32, low / len(cuts), largest / len(cuts))
        loudness = loudness * jnp.repeat(jnp.exp(heights), dims[axis_at] // parts).reshape((-1,) + (1,) * (len(dims) - 1 - axis_at))
    return loudness


def normal_values(rng, extent, scale, limit, split=(), held_as=jnp.bfloat16):
    result = jax.random.normal(rng, extent, jnp.float32) * scale
    if len(split) > 0:
        result = shard_levels(rng, extent, split, -0.22, 0.18) * result
    return jnp.clip(result, min=-limit, max=limit).astype(held_as)


def bell_draw_with(stream_key, dims, spread, reach, split, heavy, held_as=jnp.bfloat16):
    drawn = spread * jax.random.normal(stream_key, dims, jnp.float32)
    if split:
        drawn = drawn * shard_levels(stream_key, dims, split, -0.22, 0.18)
    return jnp.clip(spiked(drawn, jax.random.fold_in(stream_key, 3), *heavy), -reach, reach).astype(held_as)


def setup_inputs(seed: int = 0) -> dict:
    key_list = jax.random.split(jax.random.key(seed), 6)
    inputs = bell_draw_with(key_list[0], (N_REP, TOKENS, D), 1.0, 6.0, ((0, 4), (1, 8)), (1, 2, 8, 2.0))
    out_grad = normal_values(key_list[1], (N_REP, TOKENS, KVW), 1.0, 6.0, ((0, 4), (1, 8)))
    weight = normal_values(key_list[2], (D, KVW), 1.0, 6.0, ((0, 8),))
    momentum = normal_values(key_list[3], (N_REP, GROUPS, GROUP), 1.0, 6.0, ((0, 4), (1, 8)), jnp.float32)
    band_index = draw_band_index(jax.random.fold_in(key_list[5], 71), 0)
    return dict(inputs=inputs, out_grad=out_grad, weight=weight, momentum=momentum, band_index=band_index)


MOMENTUM_DECAY = 0.9
LEARNING_RATE = 4.0

def dct_rows(band_index, length):
    positions = lax.iota(jnp.int32, length)
    freqs = band_index.astype(jnp.int32)
    phase_int = (2 * positions[None, :] + 1) * freqs[:, None] % (4 * length)
    angles = phase_int.astype(jnp.float32) * (math.pi / (2 * length))
    row_scale = jnp.where(freqs == 0, math.sqrt(1.0 / length), math.sqrt(2.0 / length)).astype(jnp.float32)
    return row_scale[:, None] * jnp.cos(angles)

def reference(inputs, out_grad, weight, momentum, band_index):
    dct_basis = dct_rows(band_index, GROUP)
    scaling = 1.0 / math.sqrt(D)
    highest = lax.Precision.HIGHEST

    def per_replica(replica_args):
        tok_inputs, upstream, old_moment = replica_args
        gradient = jnp.dot(tok_inputs.T, upstream, preferred_element_type=jnp.float32) * scaling
        moment = MOMENTUM_DECAY * old_moment + gradient.reshape(GROUPS, GROUP)
        coeffs = jnp.dot(moment, dct_basis.T, precision=highest)
        kept = moment - jnp.dot(coeffs, dct_basis, precision=highest)
        return (kept, coeffs)
    leftover, coeffs = lax.map(per_replica, (inputs, out_grad, momentum))
    shared = lax.optimization_barrier(jnp.sum(coeffs, axis=0)) / N_REP
    update_full = jnp.dot(shared, dct_basis, precision=highest).reshape(D, KVW)
    new_weight = (weight.astype(jnp.float32) - LEARNING_RATE * update_full).astype(jnp.bfloat16)

    def project(tok_inputs):
        return (jnp.dot(tok_inputs, new_weight, preferred_element_type=jnp.float32) * scaling).astype(jnp.bfloat16)
    values = lax.map(project, inputs)
    return (leftover, new_weight, values)
```

```python
import functools
import math

import jax
import jax.numpy as jnp
from jax import lax
from jax.experimental import pallas as pl
from jax.experimental.pallas import tpu as pltpu
from jax.sharding import PartitionSpec as P

MOMENTUM_DECAY = 0.9
LEARNING_RATE = 4.0


def dct_rows(band_index, length):
    positions = lax.iota(jnp.int32, length)
    phase_int = (2 * positions[None, :] + 1) * band_index[:, None] % (4 * length)
    angles = phase_int.astype(jnp.float32) * (math.pi / (2 * length))
    row_scale = jnp.where(band_index == 0, math.sqrt(1.0 / length), math.sqrt(2.0 / length)).astype(
        jnp.float32
    )
    return row_scale[:, None] * jnp.cos(angles)


def rebuild_rows(old_rows, update_rows):
    return (old_rows.astype(jnp.float32) - LEARNING_RATE * update_rows).astype(jnp.bfloat16)


def shards(inputs, out_grad, weight, momentum, band_index):
    tok_inputs = inputs[0]
    upstream = out_grad[0]
    own_rows = weight.shape[0]
    width_out = weight.shape[1]
    group_len = momentum.shape[2]
    scaling = 1.0 / math.sqrt(tok_inputs.shape[1])
    highest = lax.Precision.HIGHEST
    own_columns = lax.all_to_all(tok_inputs, "fsdp", split_axis=1, concat_axis=0, tiled=True)
    gradient = (
        lax.dot_general(
            own_columns,
            lax.all_gather(upstream, "fsdp", axis=0, tiled=True),
            (((0,), (0,)), ((), ())),
            preferred_element_type=jnp.float32,
        )
        * scaling
    )
    moment = MOMENTUM_DECAY * momentum[0] + gradient.reshape(-1, group_len)
    dct_basis = dct_rows(band_index, group_len)
    coeffs = jnp.dot(moment, dct_basis.T, precision=highest)
    leftover = (moment - jnp.dot(coeffs, dct_basis, precision=highest))[None]
    shared = lax.psum(coeffs, "rep") / lax.axis_size("rep")
    own_update = jnp.dot(shared, dct_basis, precision=highest).reshape(own_rows, width_out)
    new_weight = rebuild_rows(weight, own_update)
    running = jnp.dot(
        tok_inputs,
        lax.all_gather(new_weight, "fsdp", axis=0, tiled=True),
        preferred_element_type=jnp.float32,
    )
    values = (running * scaling).astype(jnp.bfloat16)[None]
    return (leftover, new_weight, values)


LANES = 128
F32, BF16 = jnp.float32, jnp.bfloat16


def split_hi_lo(x):
    hi = x.astype(BF16)
    return hi, (x - hi.astype(F32)).astype(BF16)


def dot(a, b, dims=((1,), (0,))):
    return lax.dot_general(a, b, (dims, ((), ())), preferred_element_type=F32)


def dot3(a_hi, a_lo, b_hi, b_lo, dims=((1,), (0,))):
    return dot(a_hi, b_hi, dims) + dot(a_hi, b_lo, dims) + dot(a_lo, b_hi, dims)


def fill_basis(band_ref, bh, bl):
    slabs, bands, width = bh.shape
    length = slabs * width
    period = 4 * length
    freq = jnp.broadcast_to(band_ref[...].astype(F32), (LANES, bands)).T.astype(jnp.int32)
    lane = lax.broadcasted_iota(jnp.int32, (bands, LANES), 1)
    row_scale = jnp.where(freq == 0, math.sqrt(1.0 / length), math.sqrt(2.0 / length)).astype(F32)

    def angle(steps):
        centred = ((steps * freq + period // 2) & (period - 1)) - period // 2
        return centred.astype(F32) * (math.pi / (2 * length))

    fine, coarse = angle(2 * lane + 1), angle(2 * LANES * lane)
    cos_fine, sin_fine = row_scale * jnp.cos(fine), row_scale * jnp.sin(fine)
    cos_coarse, sin_coarse = jnp.cos(coarse), jnp.sin(coarse)
    for at in range(length // LANES):
        tile = cos_coarse[:, at : at + 1] * cos_fine - sin_coarse[:, at : at + 1] * sin_fine
        hi, lo = split_hi_lo(tile)
        a, col = divmod(at * LANES, width)
        bh[a, :, col : col + LANES] = hi
        bl[a, :, col : col + LANES] = lo


def kernel(
    n, reps, band_ref, x_hbm, og_hbm, w_hbm, mom_hbm, left_hbm, nw_hbm, val_hbm,
    x, oc, og, w, mom, bh, bl, perm, xa, grad, left, upd, nw, odd, even, pin, pout, vin, cz, sg, val,
    load_sem, oc_send, oc_recv, og_send, og_recv, p_send, p_recv, v_send, v_recv,
    c_send, c_recv, s_send, s_recv, out_sem,
):
    me, rep = lax.axis_index("fsdp"), lax.axis_index("rep")
    tokens, depth = x.shape
    own_rows, width = w.shape
    slabs, bands, _ = bh.shape
    groups = mom.shape[0]
    scaling = 1.0 / math.sqrt(depth)
    bits = n.bit_length() - 1

    def peer(k):
        return sum((((me // 2**b) % 2 + (k >> b) % 2) % 2) * 2**b for b in range(bits))

    def across(d):
        return lax.rem(rep + d, reps)

    def columns(which):
        return pl.ds(pl.multiple_of(which * own_rows, LANES), own_rows)

    def to_peer(k, src, dst, send, recv):
        return pltpu.make_async_remote_copy(
            src_ref=src, dst_ref=dst, send_sem=send, recv_sem=recv,
            device_id={"fsdp": peer(k)}, device_id_type=pl.DeviceIdType.MESH,
        )

    def to_rep(d, src, dst, send, recv):
        return pltpu.make_async_remote_copy(
            src_ref=src, dst_ref=dst, send_sem=send, recv_sem=recv,
            device_id={"rep": across(d)}, device_id_type=pl.DeviceIdType.MESH,
        )

    loads = [
        pltpu.make_async_copy(x_hbm.at[0], x, load_sem.at[0]),
        pltpu.make_async_copy(og_hbm.at[0], og.at[0], load_sem.at[1]),
        pltpu.make_async_copy(w_hbm, w, load_sem.at[2]),
        pltpu.make_async_copy(mom_hbm.at[0], mom, load_sem.at[3]),
        pltpu.make_async_copy(x_hbm.at[0, :, columns(me)], oc.at[0], load_sem.at[4]),
    ]
    for load in loads:
        load.start()

    barrier = pltpu.get_barrier_semaphore()
    for k in range(1, n):
        pl.semaphore_signal(
            barrier, inc=1, device_id={"fsdp": peer(k)}, device_id_type=pl.DeviceIdType.MESH
        )
    for d in range(1, reps):
        pl.semaphore_signal(
            barrier, inc=1, device_id={"rep": across(d)}, device_id_type=pl.DeviceIdType.MESH
        )
    pl.semaphore_wait(barrier, n - 1 + reps - 1)

    og_copies = {}
    for k in [k for k in range(2, n, 2)] + [1]:
        og_copies[k] = to_peer(k, og_hbm.at[0], og.at[k], og_send.at[k], og_recv.at[k])
    oc_copies = {
        k: to_peer(k, x_hbm.at[0, :, columns(peer(k))], oc.at[k], oc_send.at[k], oc_recv.at[k])
        for k in range(1, n)
    }
    order = sorted(range(2, n), key=lambda k: (-bin(k >> 1).count("1"), k % 2, k))
    for k in range(2, n, 2):
        og_copies[k].start()
    for k in order:
        oc_copies[k].start()
    og_copies[1].start()
    oc_copies[1].start()

    fill_basis(band_ref, bh, bl)

    forward = {
        k: to_peer(1, og.at[k], og.at[k + 1], og_send.at[k + 1], og_recv.at[k + 1])
        for k in range(2, n, 2)
    }
    loads[0].wait()
    span = slabs * LANES
    row = lax.broadcasted_iota(jnp.int32, (span, LANES), 0)
    lane = lax.broadcasted_iota(jnp.int32, (span, LANES), 1)
    for a in range(slabs):
        perm[:, a * LANES : (a + 1) * LANES] = (row == slabs * lane + a).astype(F32).astype(BF16)
    for piece in range(depth // span):
        sorted_piece = dot(x[:, piece * span : (piece + 1) * span], perm[...]).astype(BF16)
        for a in range(slabs):
            xa[a * tokens : (a + 1) * tokens, piece * LANES : (piece + 1) * LANES] = sorted_piece[
                :, a * LANES : (a + 1) * LANES
            ]
    for k in range(2, n, 2):
        og_copies[k].wait_recv()
        forward[k].start()

    for load in loads[1:]:
        load.wait()
    tiles = range(width // LANES)
    first = dot(oc[0], og[0], ((0,), (0,)))
    for t in tiles:
        grad[t] = first[:, t * LANES : (t + 1) * LANES]
    even[0] = dot(oc[0], w[...])
    to_partner = {}
    for k in [1] + order:
        oc_copies[k].wait_recv()
        if k % 2 and k > 1:
            forward[k - 1].wait_recv()
        elif k == 1:
            og_copies[1].wait_recv()
        product = dot(oc[k], og[k], ((0,), (0,)))
        for t in tiles:
            grad[t] += product[:, t * LANES : (t + 1) * LANES]
        partial = dot(oc[k], w[...])
        if k % 2:
            odd[k // 2] = partial.astype(BF16)
            to_partner[k] = to_peer(1, odd.at[k // 2], pin.at[k // 2], p_send.at[k // 2], p_recv.at[k // 2])
            to_partner[k].start()
        else:
            even[k // 2] = partial

    total = None
    for a in range(slabs):
        rows = [grad[t, pl.ds(a, groups, stride=slabs), :] for t in tiles]
        part = MOMENTUM_DECAY * mom[:, a * width : (a + 1) * width] + scaling * jnp.concatenate(rows, 1)
        mom[:, a * width : (a + 1) * width] = part
        hi, lo = split_hi_lo(part)
        term = dot3(hi, lo, bh[a], bl[a], ((1,), (1,)))
        total = term if total is None else total + term
    cz[rep] = total.astype(BF16)
    c_copies = [to_rep(d, cz.at[rep], cz.at[rep], c_send.at[d], c_recv.at[d]) for d in range(1, reps)]
    for c in c_copies:
        c.start()

    v_copies = []
    for h in range(1, n // 2):
        to_partner[2 * h + 1].wait_recv()
        pout[h] = (even[h] + pin[h].astype(F32)).astype(BF16)
        copy = to_peer(2 * h, pout.at[h], vin.at[h], v_send.at[h], v_recv.at[h])
        copy.start()
        v_copies.append(copy)

    c_hi, c_lo = split_hi_lo(total)
    for a in range(slabs):
        cut = slice(a * width, (a + 1) * width)
        left[:, cut] = mom[:, cut] - dot3(c_hi, c_lo, bh[a], bl[a])
    out_left = pltpu.make_async_copy(left, left_hbm.at[0], out_sem.at[0])
    out_left.start()

    for c in c_copies:
        c.wait_recv()
    shared = cz[0].astype(F32)
    for d in range(1, reps):
        shared = shared + cz[d].astype(F32)
    shared = shared / reps
    sg[me] = shared.astype(BF16)
    s_copies = [to_peer(k, sg.at[me], sg.at[me], s_send.at[k], s_recv.at[k]) for k in range(1, n)]
    for s in s_copies:
        s.start()

    s_hi, s_lo = split_hi_lo(shared)
    for a in range(slabs):
        product = dot3(s_hi, s_lo, bh[a], bl[a])
        for t in tiles:
            upd[t, pl.ds(a, groups, stride=slabs), :] = product[:, t * LANES : (t + 1) * LANES]
    for t in tiles:
        cut = slice(t * LANES, (t + 1) * LANES)
        nw[:, cut] = rebuild_rows(w[:, cut], upd[t])
    out_nw = pltpu.make_async_copy(nw, nw_hbm, out_sem.at[1])
    out_nw.start()

    to_partner[1].wait_recv()
    base = even[0] + pin[0].astype(F32)
    for h in range(1, n // 2):
        v_copies[h - 1].wait_recv()
        base = base + vin[h].astype(F32)
    for s in s_copies:
        s.wait_recv()
    mixed = dot(xa[...], sg[...].reshape(n * groups, bands))
    change = None
    for a in range(slabs):
        hi, lo = split_hi_lo(mixed[a * tokens : (a + 1) * tokens])
        term = dot3(hi, lo, bh[a], bl[a])
        change = term if change is None else change + term
    val[...] = ((base - LEARNING_RATE * change) * scaling).astype(BF16)
    out_val = pltpu.make_async_copy(val, val_hbm.at[0], out_sem.at[2])
    out_val.start()

    for k in range(1, n):
        oc_copies[k].wait_send()
        if k % 2 and k > 1:
            forward[k - 1].wait_send()
        else:
            og_copies[k].wait_send()
        if k % 2:
            to_partner[k].wait_send()
    for copy in v_copies + c_copies + s_copies:
        copy.wait_send()
    out_left.wait()
    out_nw.wait()
    out_val.wait()


def fused_shards(n, reps, inputs, out_grad, weight, momentum, band_index):
    tokens, depth = inputs.shape[1:]
    own_rows, width = weight.shape
    groups, group_len = momentum.shape[1:]
    slabs, bands = group_len // width, band_index.shape[0]
    half = n // 2
    dma = pltpu.SemaphoreType.DMA
    span = slabs * LANES
    anywhere = pl.BlockSpec(memory_space=pl.ANY)
    return pl.pallas_call(
        functools.partial(kernel, n, reps),
        out_shape=(
            jax.ShapeDtypeStruct(momentum.shape, F32),
            jax.ShapeDtypeStruct(weight.shape, BF16),
            jax.ShapeDtypeStruct(out_grad.shape, BF16),
        ),
        in_specs=[pl.BlockSpec(memory_space=pltpu.VMEM)] + [anywhere] * 4,
        out_specs=(anywhere,) * 3,
        scratch_shapes=[
            pltpu.VMEM((tokens, depth), BF16),
            pltpu.VMEM((n, tokens, own_rows), BF16),
            pltpu.VMEM((n, tokens, width), BF16),
            pltpu.VMEM((own_rows, width), BF16),
            pltpu.VMEM((groups, group_len), F32),
            pltpu.VMEM((slabs, bands, width), BF16),
            pltpu.VMEM((slabs, bands, width), BF16),
            pltpu.VMEM((span, span), BF16),
            pltpu.VMEM((slabs * tokens, depth // slabs), BF16),
            pltpu.VMEM((width // LANES, own_rows, LANES), F32),
            pltpu.VMEM((groups, group_len), F32),
            pltpu.VMEM((width // LANES, own_rows, LANES), F32),
            pltpu.VMEM((own_rows, width), BF16),
            pltpu.VMEM((half, tokens, width), BF16),
            pltpu.VMEM((half, tokens, width), F32),
            pltpu.VMEM((half, tokens, width), BF16),
            pltpu.VMEM((half, tokens, width), BF16),
            pltpu.VMEM((half, tokens, width), BF16),
            pltpu.VMEM((reps, groups, bands), BF16),
            pltpu.VMEM((n, groups, bands), BF16),
            pltpu.VMEM((tokens, width), BF16),
            dma((5,)),
            dma((n,)), dma((n,)), dma((n,)), dma((n,)),
            dma((half,)), dma((half,)), dma((half,)), dma((half,)),
            dma((reps,)), dma((reps,)), dma((n,)), dma((n,)),
            dma((3,)),
        ],
        compiler_params=pltpu.CompilerParams(collective_id=0, has_side_effects=True),
    )(band_index.reshape(1, -1), inputs, out_grad, weight, momentum)


def fits_kernel(n, inputs, weight, momentum, band_index):
    tokens, depth = inputs.shape[1:]
    own_rows, width = weight.shape
    groups, group_len = momentum.shape[1:]
    return (
        n > 1
        and n & (n - 1) == 0
        and group_len & (group_len - 1) == 0
        and tokens % 16 == 0
        and own_rows % LANES == 0
        and width % LANES == 0
        and groups % 16 == 0
        and group_len % width == 0
        and group_len // LANES <= LANES
        and depth % (group_len // width * LANES) == 0
        and band_index.shape[0] % LANES == 0
    )


def program(n, reps, inputs, out_grad, weight, momentum, band_index):
    if fits_kernel(n, inputs, weight, momentum, band_index):
        return fused_shards(n, reps, inputs, out_grad, weight, momentum, band_index)
    return shards(inputs, out_grad, weight, momentum, band_index)


def solution(mesh):
    placed = (
        P("rep", "fsdp", None),
        P("rep", "fsdp", None),
        P("fsdp", None),
        P("rep", "fsdp", None),
        P(),
    )
    return jax.shard_map(
        functools.partial(program, mesh.shape["fsdp"], mesh.shape["rep"]),
        mesh=mesh,
        in_specs=placed,
        out_specs=(P("rep", "fsdp", None), P("fsdp", None), P("rep", "fsdp", None)),
        check_vma=False,
    )
```

```python
import functools
import math

import jax
import jax.numpy as jnp
from jax import lax
from jax.experimental import pallas as pl
from jax.experimental.pallas import tpu as pltpu
from jax.sharding import PartitionSpec as P

MOMENTUM_DECAY = 0.9
LEARNING_RATE = 4.0


def dct_rows(band_index, length):
    positions = lax.iota(jnp.int32, length)
    phase_int = (2 * positions[None, :] + 1) * band_index[:, None] % (4 * length)
    angles = phase_int.astype(jnp.float32) * (math.pi / (2 * length))
    row_scale = jnp.where(band_index == 0, math.sqrt(1.0 / length), math.sqrt(2.0 / length)).astype(
        jnp.float32
    )
    return row_scale[:, None] * jnp.cos(angles)


def rebuild_rows(old_rows, update_rows):
    return (old_rows.astype(jnp.float32) - LEARNING_RATE * update_rows).astype(jnp.bfloat16)


def shards(inputs, out_grad, weight, momentum, band_index):
    tok_inputs = inputs[0]
    upstream = out_grad[0]
    own_rows = weight.shape[0]
    width_out = weight.shape[1]
    group_len = momentum.shape[2]
    scaling = 1.0 / math.sqrt(tok_inputs.shape[1])
    highest = lax.Precision.HIGHEST
    own_columns = lax.all_to_all(tok_inputs, "fsdp", split_axis=1, concat_axis=0, tiled=True)
    gradient = (
        lax.dot_general(
            own_columns,
            lax.all_gather(upstream, "fsdp", axis=0, tiled=True),
            (((0,), (0,)), ((), ())),
            preferred_element_type=jnp.float32,
        )
        * scaling
    )
    moment = MOMENTUM_DECAY * momentum[0] + gradient.reshape(-1, group_len)
    dct_basis = dct_rows(band_index, group_len)
    coeffs = jnp.dot(moment, dct_basis.T, precision=highest)
    leftover = (moment - jnp.dot(coeffs, dct_basis, precision=highest))[None]
    shared = lax.psum(coeffs, "rep") / lax.axis_size("rep")
    own_update = jnp.dot(shared, dct_basis, precision=highest).reshape(own_rows, width_out)
    new_weight = rebuild_rows(weight, own_update)
    running = jnp.dot(
        tok_inputs,
        lax.all_gather(new_weight, "fsdp", axis=0, tiled=True),
        preferred_element_type=jnp.float32,
    )
    values = (running * scaling).astype(jnp.bfloat16)[None]
    return (leftover, new_weight, values)


LANES = 128
F32, BF16 = jnp.float32, jnp.bfloat16


def split_hi_lo(x):
    hi = x.astype(BF16)
    return hi, (x - hi.astype(F32)).astype(BF16)


def dot(a, b, dims=((1,), (0,))):
    return lax.dot_general(a, b, (dims, ((), ())), preferred_element_type=F32)


def dot3(a_hi, a_lo, b_hi, b_lo, dims=((1,), (0,))):
    return dot(a_hi, b_hi, dims) + dot(a_hi, b_lo, dims) + dot(a_lo, b_hi, dims)


def fill_basis(band_ref, bh, bl, bt):
    slabs, bands, width = bh.shape
    length = slabs * width
    period = 4 * length
    freq = jnp.broadcast_to(band_ref[...].astype(F32), (LANES, bands)).T.astype(jnp.int32)
    lane = lax.broadcasted_iota(jnp.int32, (bands, LANES), 1)
    row_scale = jnp.where(freq == 0, math.sqrt(1.0 / length), math.sqrt(2.0 / length)).astype(F32)

    def angle(steps):
        centred = ((steps * freq + period // 2) & (period - 1)) - period // 2
        return centred.astype(F32) * (math.pi / (2 * length))

    fine, coarse = angle(2 * lane + 1), angle(2 * LANES * lane)
    cos_fine, sin_fine = row_scale * jnp.cos(fine), row_scale * jnp.sin(fine)
    cos_coarse, sin_coarse = jnp.cos(coarse), jnp.sin(coarse)
    for at in range(length // LANES):
        tile = cos_coarse[:, at : at + 1] * cos_fine - sin_coarse[:, at : at + 1] * sin_fine
        hi, lo = split_hi_lo(tile)
        a, col = divmod(at * LANES, width)
        bh[a, :, col : col + LANES] = hi
        bl[a, :, col : col + LANES] = lo
        hi, lo = split_hi_lo(tile.T)
        bt[at * LANES : (at + 1) * LANES, :bands] = hi
        bt[at * LANES : (at + 1) * LANES, bands:] = lo


def kernel(
    n, reps, band_ref, x_hbm, og_hbm, w_hbm, mom_hbm, left, nw, val,
    x, oc, og, w, mom, bh, bl, bt, perm, xa, grad, upd, odd, even, pin, pout, vin, cz, sg,
    load_sem, oc_send, oc_recv, og_send, og_recv, p_send, p_recv, v_send, v_recv,
    c_send, c_recv, s_send, s_recv,
):
    me, rep = lax.axis_index("fsdp"), lax.axis_index("rep")
    tokens, depth = x.shape
    own_rows, width = w.shape
    slabs, bands, _ = bh.shape
    groups = mom.shape[0]
    scaling = 1.0 / math.sqrt(depth)
    bits = n.bit_length() - 1

    def peer(k):
        return sum((((me // 2**b) % 2 + (k >> b) % 2) % 2) * 2**b for b in range(bits))

    def across(d):
        return lax.rem(rep + d, reps)

    def columns(which):
        return pl.ds(pl.multiple_of(which * own_rows, LANES), own_rows)

    def to_peer(k, src, dst, send, recv):
        return pltpu.make_async_remote_copy(
            src_ref=src, dst_ref=dst, send_sem=send, recv_sem=recv,
            device_id={"fsdp": peer(k)}, device_id_type=pl.DeviceIdType.MESH,
        )

    def to_rep(d, src, dst, send, recv):
        return pltpu.make_async_remote_copy(
            src_ref=src, dst_ref=dst, send_sem=send, recv_sem=recv,
            device_id={"rep": across(d)}, device_id_type=pl.DeviceIdType.MESH,
        )

    loads = [
        pltpu.make_async_copy(x_hbm.at[0], x, load_sem.at[0]),
        pltpu.make_async_copy(og_hbm.at[0], og.at[0], load_sem.at[1]),
        pltpu.make_async_copy(w_hbm, w, load_sem.at[2]),
        pltpu.make_async_copy(mom_hbm.at[0], mom, load_sem.at[3]),
        pltpu.make_async_copy(x_hbm.at[0, :, columns(me)], oc.at[0], load_sem.at[4]),
    ]
    for load in loads:
        load.start()

    barrier = pltpu.get_barrier_semaphore()
    for k in range(1, n):
        pl.semaphore_signal(
            barrier, inc=1, device_id={"fsdp": peer(k)}, device_id_type=pl.DeviceIdType.MESH
        )
    for d in range(1, reps):
        pl.semaphore_signal(
            barrier, inc=1, device_id={"rep": across(d)}, device_id_type=pl.DeviceIdType.MESH
        )
    pl.semaphore_wait(barrier, n - 1 + reps - 1)

    og_copies = {}
    for k in [k for k in range(2, n, 2)] + [1]:
        og_copies[k] = to_peer(k, og_hbm.at[0], og.at[k], og_send.at[k], og_recv.at[k])
    oc_copies = {
        k: to_peer(k, x_hbm.at[0, :, columns(peer(k))], oc.at[k], oc_send.at[k], oc_recv.at[k])
        for k in range(1, n)
    }
    order = sorted(range(2, n), key=lambda k: (-bin(k >> 1).count("1"), k % 2, k))
    for k in range(2, n, 2):
        og_copies[k].start()
    for k in order:
        oc_copies[k].start()
    og_copies[1].start()
    oc_copies[1].start()

    fill_basis(band_ref, bh, bl, bt)

    forward = {
        k: to_peer(1, og.at[k], og.at[k + 1], og_send.at[k + 1], og_recv.at[k + 1])
        for k in range(2, n, 2)
    }
    loads[0].wait()
    span = slabs * LANES
    row = lax.broadcasted_iota(jnp.int32, (span, LANES), 0)
    lane = lax.broadcasted_iota(jnp.int32, (span, LANES), 1)
    for a in range(slabs):
        perm[:, a * LANES : (a + 1) * LANES] = (row == slabs * lane + a).astype(F32).astype(BF16)
    for piece in range(depth // span):
        sorted_piece = dot(x[:, piece * span : (piece + 1) * span], perm[...]).astype(BF16)
        for a in range(slabs):
            xa[a * tokens : (a + 1) * tokens, piece * LANES : (piece + 1) * LANES] = sorted_piece[
                :, a * LANES : (a + 1) * LANES
            ]
    for k in range(2, n, 2):
        og_copies[k].wait_recv()
        forward[k].start()

    for load in loads[1:]:
        load.wait()
    tiles = range(width // LANES)
    first = dot(oc[0], og[0], ((0,), (0,)))
    for t in tiles:
        grad[t] = first[:, t * LANES : (t + 1) * LANES]
    even[0] = dot(oc[0], w[...])
    to_partner = {}
    for k in [1] + order:
        oc_copies[k].wait_recv()
        if k % 2 and k > 1:
            forward[k - 1].wait_recv()
        elif k == 1:
            og_copies[1].wait_recv()
        product = dot(oc[k], og[k], ((0,), (0,)))
        for t in tiles:
            grad[t] += product[:, t * LANES : (t + 1) * LANES]
        partial = dot(oc[k], w[...])
        if k % 2:
            odd[k // 2] = partial.astype(BF16)
            to_partner[k] = to_peer(1, odd.at[k // 2], pin.at[k // 2], p_send.at[k // 2], p_recv.at[k // 2])
            to_partner[k].start()
        else:
            even[k // 2] = partial

    v_copies = []
    for h in range(1, n // 2):
        to_partner[2 * h + 1].wait_recv()
        pout[h] = (even[h] + pin[h].astype(F32)).astype(BF16)
        copy = to_peer(2 * h, pout.at[h], vin.at[h], v_send.at[h], v_recv.at[h])
        copy.start()
        v_copies.append(copy)

    wide, narrow = None, None
    for a in range(slabs):
        rows = [grad[t, pl.ds(a, groups, stride=slabs), :] for t in tiles]
        part = MOMENTUM_DECAY * mom[:, a * width : (a + 1) * width] + scaling * jnp.concatenate(rows, 1)
        mom[:, a * width : (a + 1) * width] = part
        hi, lo = split_hi_lo(part)
        both = dot(hi, bt[a * width : (a + 1) * width, :])
        rest = dot(lo, bt[a * width : (a + 1) * width, :bands])
        wide = both if wide is None else wide + both
        narrow = rest if narrow is None else narrow + rest
    total = wide[:, :bands] + (wide[:, bands:] + narrow)
    cz[rep] = total.astype(BF16)
    c_copies = [to_rep(d, cz.at[rep], cz.at[rep], c_send.at[d], c_recv.at[d]) for d in range(1, reps)]
    for c in c_copies:
        c.start()

    c_hi, c_lo = split_hi_lo(total)
    for a in range(slabs):
        cut = slice(a * width, (a + 1) * width)
        left[0, :, cut] = mom[:, cut] - dot3(c_hi, c_lo, bh[a], bl[a])

    for c in c_copies:
        c.wait_recv()
    shared = cz[0].astype(F32)
    for d in range(1, reps):
        shared = shared + cz[d].astype(F32)
    shared = shared / reps
    sg[me] = shared.astype(BF16)
    s_copies = [to_peer(k, sg.at[me], sg.at[me], s_send.at[k], s_recv.at[k]) for k in range(1, n)]
    for s in s_copies:
        s.start()

    s_hi, s_lo = split_hi_lo(shared)
    for a in range(slabs):
        product = dot3(s_hi, s_lo, bh[a], bl[a])
        for t in tiles:
            upd[t, pl.ds(a, groups, stride=slabs), :] = product[:, t * LANES : (t + 1) * LANES]
    for t in tiles:
        cut = slice(t * LANES, (t + 1) * LANES)
        nw[:, cut] = rebuild_rows(w[:, cut], upd[t])

    to_partner[1].wait_recv()
    base = even[0] + pin[0].astype(F32)
    for h in range(1, n // 2):
        v_copies[h - 1].wait_recv()
        base = base + vin[h].astype(F32)
    for s in s_copies:
        s.wait_recv()
    mixed = dot(xa[...], sg[...].reshape(n * groups, bands))
    mixed = jnp.concatenate([mixed[a * tokens : (a + 1) * tokens] for a in range(slabs)], 1)
    hi, lo = split_hi_lo(mixed)
    change = dot3(hi, lo, bh[...].reshape(slabs * bands, width), bl[...].reshape(slabs * bands, width))
    val[0] = ((base - LEARNING_RATE * change) * scaling).astype(BF16)

    for k in range(1, n):
        oc_copies[k].wait_send()
        if k % 2 and k > 1:
            forward[k - 1].wait_send()
        else:
            og_copies[k].wait_send()
        if k % 2:
            to_partner[k].wait_send()
    for copy in v_copies + c_copies + s_copies:
        copy.wait_send()


def fused_shards(n, reps, inputs, out_grad, weight, momentum, band_index):
    tokens, depth = inputs.shape[1:]
    own_rows, width = weight.shape
    groups, group_len = momentum.shape[1:]
    slabs, bands = group_len // width, band_index.shape[0]
    half = n // 2
    dma = pltpu.SemaphoreType.DMA
    span = slabs * LANES
    anywhere = pl.BlockSpec(memory_space=pl.ANY)
    return pl.pallas_call(
        functools.partial(kernel, n, reps),
        out_shape=(
            pltpu.VMEM(momentum.shape, F32),
            pltpu.VMEM(weight.shape, BF16),
            pltpu.VMEM(out_grad.shape, BF16),
        ),
        in_specs=[pl.BlockSpec(memory_space=pltpu.VMEM)] + [anywhere] * 4,
        out_specs=(pl.BlockSpec(memory_space=pltpu.VMEM),) * 3,
        scratch_shapes=[
            pltpu.VMEM((tokens, depth), BF16),
            pltpu.VMEM((n, tokens, own_rows), BF16),
            pltpu.VMEM((n, tokens, width), BF16),
            pltpu.VMEM((own_rows, width), BF16),
            pltpu.VMEM((groups, group_len), F32),
            pltpu.VMEM((slabs, bands, width), BF16),
            pltpu.VMEM((slabs, bands, width), BF16),
            pltpu.VMEM((group_len, 2 * bands), BF16),
            pltpu.VMEM((span, span), BF16),
            pltpu.VMEM((slabs * tokens, depth // slabs), BF16),
            pltpu.VMEM((width // LANES, own_rows, LANES), F32),
            pltpu.VMEM((width // LANES, own_rows, LANES), F32),
            pltpu.VMEM((half, tokens, width), BF16),
            pltpu.VMEM((half, tokens, width), F32),
            pltpu.VMEM((half, tokens, width), BF16),
            pltpu.VMEM((half, tokens, width), BF16),
            pltpu.VMEM((half, tokens, width), BF16),
            pltpu.VMEM((reps, groups, bands), BF16),
            pltpu.VMEM((n, groups, bands), BF16),
            dma((5,)),
            dma((n,)), dma((n,)), dma((n,)), dma((n,)),
            dma((half,)), dma((half,)), dma((half,)), dma((half,)),
            dma((reps,)), dma((reps,)), dma((n,)), dma((n,)),
        ],
        compiler_params=pltpu.CompilerParams(collective_id=0, has_side_effects=True),
    )(band_index.reshape(1, -1), inputs, out_grad, weight, momentum)


def fits_kernel(n, inputs, weight, momentum, band_index):
    tokens, depth = inputs.shape[1:]
    own_rows, width = weight.shape
    groups, group_len = momentum.shape[1:]
    return (
        n > 1
        and n & (n - 1) == 0
        and group_len & (group_len - 1) == 0
        and tokens % 16 == 0
        and own_rows % LANES == 0
        and width % LANES == 0
        and groups % 16 == 0
        and group_len % width == 0
        and group_len // LANES <= LANES
        and depth % (group_len // width * LANES) == 0
        and band_index.shape[0] % LANES == 0
    )


def program(n, reps, inputs, out_grad, weight, momentum, band_index):
    if fits_kernel(n, inputs, weight, momentum, band_index):
        return fused_shards(n, reps, inputs, out_grad, weight, momentum, band_index)
    return shards(inputs, out_grad, weight, momentum, band_index)


def solution(mesh):
    placed = (
        P("rep", "fsdp", None),
        P("rep", "fsdp", None),
        P("fsdp", None),
        P("rep", "fsdp", None),
        P(),
    )
    return jax.shard_map(
        functools.partial(program, mesh.shape["fsdp"], mesh.shape["rep"]),
        mesh=mesh,
        in_specs=placed,
        out_specs=(P("rep", "fsdp", None), P("fsdp", None), P("rep", "fsdp", None)),
        check_vma=False,
    )
```

```python
import functools
import math

import jax
import jax.numpy as jnp
from jax import lax
from jax.experimental import pallas as pl
from jax.experimental.pallas import tpu as pltpu
from jax.sharding import PartitionSpec as P

MOMENTUM_DECAY = 0.9
LEARNING_RATE = 4.0


def dct_rows(band_index, length):
    positions = lax.iota(jnp.int32, length)
    phase_int = (2 * positions[None, :] + 1) * band_index[:, None] % (4 * length)
    angles = phase_int.astype(jnp.float32) * (math.pi / (2 * length))
    row_scale = jnp.where(band_index == 0, math.sqrt(1.0 / length), math.sqrt(2.0 / length)).astype(
        jnp.float32
    )
    return row_scale[:, None] * jnp.cos(angles)


def rebuild_rows(old_rows, update_rows):
    return (old_rows.astype(jnp.float32) - LEARNING_RATE * update_rows).astype(jnp.bfloat16)


def shards(inputs, out_grad, weight, momentum, band_index):
    tok_inputs = inputs[0]
    upstream = out_grad[0]
    own_rows = weight.shape[0]
    width_out = weight.shape[1]
    group_len = momentum.shape[2]
    scaling = 1.0 / math.sqrt(tok_inputs.shape[1])
    highest = lax.Precision.HIGHEST
    own_columns = lax.all_to_all(tok_inputs, "fsdp", split_axis=1, concat_axis=0, tiled=True)
    gradient = (
        lax.dot_general(
            own_columns,
            lax.all_gather(upstream, "fsdp", axis=0, tiled=True),
            (((0,), (0,)), ((), ())),
            preferred_element_type=jnp.float32,
        )
        * scaling
    )
    moment = MOMENTUM_DECAY * momentum[0] + gradient.reshape(-1, group_len)
    dct_basis = dct_rows(band_index, group_len)
    coeffs = jnp.dot(moment, dct_basis.T, precision=highest)
    leftover = (moment - jnp.dot(coeffs, dct_basis, precision=highest))[None]
    shared = lax.psum(coeffs, "rep") / lax.axis_size("rep")
    own_update = jnp.dot(shared, dct_basis, precision=highest).reshape(own_rows, width_out)
    new_weight = rebuild_rows(weight, own_update)
    running = jnp.dot(
        tok_inputs,
        lax.all_gather(new_weight, "fsdp", axis=0, tiled=True),
        preferred_element_type=jnp.float32,
    )
    values = (running * scaling).astype(jnp.bfloat16)[None]
    return (leftover, new_weight, values)


LANES = 128
F32, BF16 = jnp.float32, jnp.bfloat16


def split_hi_lo(x):
    hi = x.astype(BF16)
    return hi, (x - hi.astype(F32)).astype(BF16)


def dot(a, b, dims=((1,), (0,))):
    return lax.dot_general(a, b, (dims, ((), ())), preferred_element_type=F32)


def dot3(a_hi, a_lo, b_hi, b_lo, dims=((1,), (0,))):
    return dot(a_hi, b_hi, dims) + dot(a_hi, b_lo, dims) + dot(a_lo, b_hi, dims)


def fill_basis(band_ref, bh, bl, bt):
    slabs, bands, width = bh.shape
    length = slabs * width
    period = 4 * length
    freq = jnp.broadcast_to(band_ref[...].astype(F32), (LANES, bands)).T.astype(jnp.int32)
    lane = lax.broadcasted_iota(jnp.int32, (bands, LANES), 1)
    row_scale = jnp.where(freq == 0, math.sqrt(1.0 / length), math.sqrt(2.0 / length)).astype(F32)

    def angle(steps):
        centred = ((steps * freq + period // 2) & (period - 1)) - period // 2
        return centred.astype(F32) * (math.pi / (2 * length))

    fine, coarse = angle(2 * lane + 1), angle(2 * LANES * lane)
    cos_fine, sin_fine = row_scale * jnp.cos(fine), row_scale * jnp.sin(fine)
    cos_coarse, sin_coarse = jnp.cos(coarse), jnp.sin(coarse)
    for at in range(length // LANES):
        tile = cos_coarse[:, at : at + 1] * cos_fine - sin_coarse[:, at : at + 1] * sin_fine
        hi, lo = split_hi_lo(tile)
        a, col = divmod(at * LANES, width)
        bh[a, :, col : col + LANES] = hi
        bl[a, :, col : col + LANES] = lo
        hi, lo = split_hi_lo(tile.T)
        bt[at * LANES : (at + 1) * LANES, :bands] = hi
        bt[at * LANES : (at + 1) * LANES, bands:] = lo


def kernel(
    n, reps, band_ref, x_hbm, og_hbm, w_hbm, mom_hbm, left, nw, val,
    x, oc, og, w, mom, bh, bl, bt, perm, xa, grad, upd, odd, even, pin, pout, vin, cz, sg,
    load_sem, oc_send, oc_recv, og_send, og_recv, r_send, r_recv, p_send, p_recv, v_send, v_recv,
    c_send, c_recv, s_send, s_recv,
):
    me, rep = lax.axis_index("fsdp"), lax.axis_index("rep")
    tokens, depth = x.shape
    own_rows, width = w.shape
    slabs, bands, _ = bh.shape
    groups = mom.shape[0]
    scaling = 1.0 / math.sqrt(depth)
    bits = n.bit_length() - 1

    def peer(k):
        return sum((((me // 2**b) % 2 + (k >> b) % 2) % 2) * 2**b for b in range(bits))

    def across(d):
        return lax.rem(rep + d, reps)

    def columns(which):
        return pl.ds(pl.multiple_of(which * own_rows, LANES), own_rows)

    def to_peer(k, src, dst, send, recv):
        return pltpu.make_async_remote_copy(
            src_ref=src, dst_ref=dst, send_sem=send, recv_sem=recv,
            device_id={"fsdp": peer(k)}, device_id_type=pl.DeviceIdType.MESH,
        )

    def to_rep(d, src, dst, send, recv):
        return pltpu.make_async_remote_copy(
            src_ref=src, dst_ref=dst, send_sem=send, recv_sem=recv,
            device_id={"rep": across(d)}, device_id_type=pl.DeviceIdType.MESH,
        )

    loads = [
        pltpu.make_async_copy(x_hbm.at[0], x, load_sem.at[0]),
        pltpu.make_async_copy(og_hbm.at[0], og.at[0], load_sem.at[1]),
        pltpu.make_async_copy(w_hbm, w, load_sem.at[2]),
        pltpu.make_async_copy(mom_hbm.at[0], mom, load_sem.at[3]),
        pltpu.make_async_copy(x_hbm.at[0, :, columns(me)], oc.at[0], load_sem.at[4]),
    ]
    for load in loads:
        load.start()

    barrier = pltpu.get_barrier_semaphore()
    for d in range(1, reps):
        pl.semaphore_signal(
            barrier, inc=1, device_id={"rep": across(d)}, device_id_type=pl.DeviceIdType.MESH
        )
    for k in range(n - 1, 0, -1):
        pl.semaphore_signal(
            barrier, inc=1, device_id={"fsdp": peer(k)}, device_id_type=pl.DeviceIdType.MESH
        )
    pl.semaphore_wait(barrier, n - 1 + reps - 1)

    def crossings(k):
        return bin(k >> 1).count("1")

    relayed = [k for k in range(2, n, 2) if crossings(k) == 2]
    direct = [k for k in range(2, n, 2) if k not in relayed]
    order = sorted(range(2, n), key=lambda k: (-crossings(k), k % 2, k))
    og_copies = {
        k: to_peer(k, og_hbm.at[0], og.at[k], og_send.at[k], og_recv.at[k]) for k in direct + [1]
    }
    oc_copies = {
        k: to_peer(k, x_hbm.at[0, :, columns(peer(k))], oc.at[k], oc_send.at[k], oc_recv.at[k])
        for k in range(1, n)
    }
    forward = {
        k: to_peer(1, og.at[k], og.at[k + 1], og_send.at[k + 1], og_recv.at[k + 1])
        for k in range(2, n, 2)
    }
    relays = {}
    for k in relayed:
        low = k & -k
        for side, via in enumerate((low, k - low)):
            part = pl.ds(side * (tokens // 2), tokens // 2)
            relays[k, side] = to_peer(
                via, og.at[k - via, part], og.at[k, part], r_send.at[k, side], r_recv.at[k, side]
            )
    for copy in og_copies.values():
        copy.start()
    early = [k for k in order if crossings(k) > 1] + [1]
    for k in early:
        oc_copies[k].start()

    fill_basis(band_ref, bh, bl, bt)

    for k in direct:
        og_copies[k].wait_recv()
    for copy in relays.values():
        copy.start()
    for k in order:
        if k not in early:
            oc_copies[k].start()
    for k in direct:
        forward[k].start()

    loads[0].wait()
    span = slabs * LANES
    row = lax.broadcasted_iota(jnp.int32, (span, LANES), 0)
    lane = lax.broadcasted_iota(jnp.int32, (span, LANES), 1)
    for a in range(slabs):
        perm[:, a * LANES : (a + 1) * LANES] = (row == slabs * lane + a).astype(F32).astype(BF16)
    for piece in range(depth // span):
        sorted_piece = dot(x[:, piece * span : (piece + 1) * span], perm[...]).astype(BF16)
        for a in range(slabs):
            xa[a * tokens : (a + 1) * tokens, piece * LANES : (piece + 1) * LANES] = sorted_piece[
                :, a * LANES : (a + 1) * LANES
            ]
    for k in relayed:
        relays[k, 0].wait_recv()
        relays[k, 1].wait_recv()
        forward[k].start()

    for load in loads[1:]:
        load.wait()
    tiles = range(width // LANES)
    first = dot(oc[0], og[0], ((0,), (0,)))
    for t in tiles:
        grad[t] = first[:, t * LANES : (t + 1) * LANES]
    even[0] = dot(oc[0], w[...])
    to_partner = {}
    for k in [1] + order:
        oc_copies[k].wait_recv()
        if k % 2 and k > 1:
            forward[k - 1].wait_recv()
        elif k == 1:
            og_copies[1].wait_recv()
        product = dot(oc[k], og[k], ((0,), (0,)))
        for t in tiles:
            grad[t] += product[:, t * LANES : (t + 1) * LANES]
        partial = dot(oc[k], w[...])
        if k % 2:
            odd[k // 2] = partial.astype(BF16)
            to_partner[k] = to_peer(1, odd.at[k // 2], pin.at[k // 2], p_send.at[k // 2], p_recv.at[k // 2])
            to_partner[k].start()
        else:
            even[k // 2] = partial

    v_copies = []
    for h in range(1, n // 2):
        to_partner[2 * h + 1].wait_recv()
        pout[h] = (even[h] + pin[h].astype(F32)).astype(BF16)
        copy = to_peer(2 * h, pout.at[h], vin.at[h], v_send.at[h], v_recv.at[h])
        copy.start()
        v_copies.append(copy)

    wide, narrow = None, None
    for a in range(slabs):
        rows = [grad[t, pl.ds(a, groups, stride=slabs), :] for t in tiles]
        part = MOMENTUM_DECAY * mom[:, a * width : (a + 1) * width] + scaling * jnp.concatenate(rows, 1)
        mom[:, a * width : (a + 1) * width] = part
        hi, lo = split_hi_lo(part)
        both = dot(hi, bt[a * width : (a + 1) * width, :])
        rest = dot(lo, bt[a * width : (a + 1) * width, :bands])
        wide = both if wide is None else wide + both
        narrow = rest if narrow is None else narrow + rest
    total = wide[:, :bands] + (wide[:, bands:] + narrow)
    cz[rep] = total.astype(BF16)
    c_copies = [to_rep(d, cz.at[rep], cz.at[rep], c_send.at[d], c_recv.at[d]) for d in range(1, reps)]
    for c in c_copies:
        c.start()

    c_hi, c_lo = split_hi_lo(total)
    for a in range(slabs):
        cut = slice(a * width, (a + 1) * width)
        left[0, :, cut] = mom[:, cut] - dot3(c_hi, c_lo, bh[a], bl[a])

    for c in c_copies:
        c.wait_recv()
    shared = cz[0].astype(F32)
    for d in range(1, reps):
        shared = shared + cz[d].astype(F32)
    shared = shared / reps
    sg[me] = shared.astype(BF16)
    s_copies = [to_peer(k, sg.at[me], sg.at[me], s_send.at[k], s_recv.at[k]) for k in range(1, n)]
    for s in s_copies:
        s.start()

    s_hi, s_lo = split_hi_lo(shared)
    for a in range(slabs):
        product = dot3(s_hi, s_lo, bh[a], bl[a])
        for t in tiles:
            upd[t, pl.ds(a, groups, stride=slabs), :] = product[:, t * LANES : (t + 1) * LANES]
    for t in tiles:
        cut = slice(t * LANES, (t + 1) * LANES)
        nw[:, cut] = rebuild_rows(w[:, cut], upd[t])

    to_partner[1].wait_recv()
    base = even[0] + pin[0].astype(F32)
    for h in range(1, n // 2):
        v_copies[h - 1].wait_recv()
        base = base + vin[h].astype(F32)
    for s in s_copies:
        s.wait_recv()
    mixed = dot(xa[...], sg[...].reshape(n * groups, bands))
    mixed = jnp.concatenate([mixed[a * tokens : (a + 1) * tokens] for a in range(slabs)], 1)
    hi, lo = split_hi_lo(mixed)
    change = dot3(hi, lo, bh[...].reshape(slabs * bands, width), bl[...].reshape(slabs * bands, width))
    val[0] = ((base - LEARNING_RATE * change) * scaling).astype(BF16)

    for k in range(1, n):
        oc_copies[k].wait_send()
        if k % 2 and k > 1:
            forward[k - 1].wait_send()
        elif k in relayed:
            relays[k, 0].wait_send()
            relays[k, 1].wait_send()
        else:
            og_copies[k].wait_send()
        if k % 2:
            to_partner[k].wait_send()
    for copy in v_copies + c_copies + s_copies:
        copy.wait_send()


def store_kernel(left, nw, val, left_hbm, nw_hbm, val_hbm, sems):
    copies = [
        pltpu.make_async_copy(src, dst, sems.at[i])
        for i, (src, dst) in enumerate(((left, left_hbm), (nw, nw_hbm), (val, val_hbm)))
    ]
    for copy in copies:
        copy.start()
    for copy in copies:
        copy.wait()


def fused_shards(n, reps, inputs, out_grad, weight, momentum, band_index):
    tokens, depth = inputs.shape[1:]
    own_rows, width = weight.shape
    groups, group_len = momentum.shape[1:]
    slabs, bands = group_len // width, band_index.shape[0]
    half = n // 2
    dma = pltpu.SemaphoreType.DMA
    span = slabs * LANES
    anywhere = pl.BlockSpec(memory_space=pl.ANY)
    held = pl.pallas_call(
        functools.partial(kernel, n, reps),
        out_shape=(
            pltpu.VMEM(momentum.shape, F32),
            pltpu.VMEM(weight.shape, BF16),
            pltpu.VMEM(out_grad.shape, BF16),
        ),
        in_specs=[pl.BlockSpec(memory_space=pltpu.VMEM)] + [anywhere] * 4,
        out_specs=(pl.BlockSpec(memory_space=pltpu.VMEM),) * 3,
        scratch_shapes=[
            pltpu.VMEM((tokens, depth), BF16),
            pltpu.VMEM((n, tokens, own_rows), BF16),
            pltpu.VMEM((n, tokens, width), BF16),
            pltpu.VMEM((own_rows, width), BF16),
            pltpu.VMEM((groups, group_len), F32),
            pltpu.VMEM((slabs, bands, width), BF16),
            pltpu.VMEM((slabs, bands, width), BF16),
            pltpu.VMEM((group_len, 2 * bands), BF16),
            pltpu.VMEM((span, span), BF16),
            pltpu.VMEM((slabs * tokens, depth // slabs), BF16),
            pltpu.VMEM((width // LANES, own_rows, LANES), F32),
            pltpu.VMEM((width // LANES, own_rows, LANES), F32),
            pltpu.VMEM((half, tokens, width), BF16),
            pltpu.VMEM((half, tokens, width), F32),
            pltpu.VMEM((half, tokens, width), BF16),
            pltpu.VMEM((half, tokens, width), BF16),
            pltpu.VMEM((half, tokens, width), BF16),
            pltpu.VMEM((reps, groups, bands), BF16),
            pltpu.VMEM((n, groups, bands), BF16),
            dma((5,)),
            dma((n,)), dma((n,)), dma((n,)), dma((n,)), dma((n, 2)), dma((n, 2)),
            dma((half,)), dma((half,)), dma((half,)), dma((half,)),
            dma((reps,)), dma((reps,)), dma((n,)), dma((n,)),
        ],
        compiler_params=pltpu.CompilerParams(collective_id=0, has_side_effects=True),
    )(band_index.reshape(1, -1), inputs, out_grad, weight, momentum)
    return pl.pallas_call(
        store_kernel,
        out_shape=tuple(jax.ShapeDtypeStruct(a.shape, a.dtype) for a in held),
        in_specs=[anywhere] * 3,
        out_specs=(anywhere,) * 3,
        scratch_shapes=[dma((3,))],
        compiler_params=pltpu.CompilerParams(vmem_limit_bytes=1 << 20),
    )(*held)


def fits_kernel(n, inputs, weight, momentum, band_index):
    tokens, depth = inputs.shape[1:]
    own_rows, width = weight.shape
    groups, group_len = momentum.shape[1:]
    return (
        n > 1
        and n & (n - 1) == 0
        and group_len & (group_len - 1) == 0
        and tokens % 32 == 0
        and own_rows % LANES == 0
        and width % LANES == 0
        and groups % 16 == 0
        and group_len % width == 0
        and group_len // LANES <= LANES
        and depth % (group_len // width * LANES) == 0
        and band_index.shape[0] % LANES == 0
    )


def program(n, reps, inputs, out_grad, weight, momentum, band_index):
    if fits_kernel(n, inputs, weight, momentum, band_index):
        return fused_shards(n, reps, inputs, out_grad, weight, momentum, band_index)
    return shards(inputs, out_grad, weight, momentum, band_index)


def solution(mesh):
    placed = (
        P("rep", "fsdp", None),
        P("rep", "fsdp", None),
        P("fsdp", None),
        P("rep", "fsdp", None),
        P(),
    )
    return jax.shard_map(
        functools.partial(program, mesh.shape["fsdp"], mesh.shape["rep"]),
        mesh=mesh,
        in_specs=placed,
        out_specs=(P("rep", "fsdp", None), P("fsdp", None), P("rep", "fsdp", None)),
        check_vma=False,
    )
```

```python
import functools
import math

import jax
import jax.numpy as jnp
from jax import lax
from jax.experimental import pallas as pl
from jax.experimental.pallas import tpu as pltpu
from jax.sharding import PartitionSpec as P

MOMENTUM_DECAY = 0.9
LEARNING_RATE = 4.0


def dct_rows(band_index, length):
    positions = lax.iota(jnp.int32, length)
    phase_int = (2 * positions[None, :] + 1) * band_index[:, None] % (4 * length)
    angles = phase_int.astype(jnp.float32) * (math.pi / (2 * length))
    row_scale = jnp.where(band_index == 0, math.sqrt(1.0 / length), math.sqrt(2.0 / length)).astype(
        jnp.float32
    )
    return row_scale[:, None] * jnp.cos(angles)


def rebuild_rows(old_rows, update_rows):
    return (old_rows.astype(jnp.float32) - LEARNING_RATE * update_rows).astype(jnp.bfloat16)


def shards(inputs, out_grad, weight, momentum, band_index):
    tok_inputs = inputs[0]
    upstream = out_grad[0]
    own_rows = weight.shape[0]
    width_out = weight.shape[1]
    group_len = momentum.shape[2]
    scaling = 1.0 / math.sqrt(tok_inputs.shape[1])
    highest = lax.Precision.HIGHEST
    own_columns = lax.all_to_all(tok_inputs, "fsdp", split_axis=1, concat_axis=0, tiled=True)
    gradient = (
        lax.dot_general(
            own_columns,
            lax.all_gather(upstream, "fsdp", axis=0, tiled=True),
            (((0,), (0,)), ((), ())),
            preferred_element_type=jnp.float32,
        )
        * scaling
    )
    moment = MOMENTUM_DECAY * momentum[0] + gradient.reshape(-1, group_len)
    dct_basis = dct_rows(band_index, group_len)
    coeffs = jnp.dot(moment, dct_basis.T, precision=highest)
    leftover = (moment - jnp.dot(coeffs, dct_basis, precision=highest))[None]
    shared = lax.psum(coeffs, "rep") / lax.axis_size("rep")
    own_update = jnp.dot(shared, dct_basis, precision=highest).reshape(own_rows, width_out)
    new_weight = rebuild_rows(weight, own_update)
    running = jnp.dot(
        tok_inputs,
        lax.all_gather(new_weight, "fsdp", axis=0, tiled=True),
        preferred_element_type=jnp.float32,
    )
    values = (running * scaling).astype(jnp.bfloat16)[None]
    return (leftover, new_weight, values)


LANES = 128
F32, BF16 = jnp.float32, jnp.bfloat16


def split_hi_lo(x):
    hi = x.astype(BF16)
    return hi, (x - hi.astype(F32)).astype(BF16)


def dot(a, b, dims=((1,), (0,))):
    return lax.dot_general(a, b, (dims, ((), ())), preferred_element_type=F32)


def dot3(a_hi, a_lo, b_hi, b_lo, dims=((1,), (0,))):
    return dot(a_hi, b_hi, dims) + dot(a_hi, b_lo, dims) + dot(a_lo, b_hi, dims)


def fill_basis(band_ref, bh, bl, bt):
    slabs, bands, width = bh.shape
    length = slabs * width
    period = 4 * length
    freq = jnp.broadcast_to(band_ref[...].astype(F32), (LANES, bands)).T.astype(jnp.int32)
    lane = lax.broadcasted_iota(jnp.int32, (bands, LANES), 1)
    row_scale = jnp.where(freq == 0, math.sqrt(1.0 / length), math.sqrt(2.0 / length)).astype(F32)

    def angle(steps):
        centred = ((steps * freq + period // 2) & (period - 1)) - period // 2
        return centred.astype(F32) * (math.pi / (2 * length))

    fine, coarse = angle(2 * lane + 1), angle(2 * LANES * lane)
    cos_fine, sin_fine = row_scale * jnp.cos(fine), row_scale * jnp.sin(fine)
    cos_coarse, sin_coarse = jnp.cos(coarse), jnp.sin(coarse)
    for at in range(length // LANES):
        tile = cos_coarse[:, at : at + 1] * cos_fine - sin_coarse[:, at : at + 1] * sin_fine
        hi, lo = split_hi_lo(tile)
        a, col = divmod(at * LANES, width)
        bh[a, :, col : col + LANES] = hi
        bl[a, :, col : col + LANES] = lo
        hi, lo = split_hi_lo(tile.T)
        bt[at * LANES : (at + 1) * LANES, :bands] = hi
        bt[at * LANES : (at + 1) * LANES, bands:] = lo


def kernel(
    n, reps, band_ref, x_hbm, og_hbm, w_hbm, mom_hbm, left, nw, val,
    x, oc, og, w, mom, bh, bl, bt, perm, xa, grad, upd, odd, even, pin, pout, vin, cz, sg,
    load_sem, oc_send, oc_recv, og_send, og_recv, r_send, r_recv, p_send, p_recv, v_send, v_recv,
    c_send, c_recv, s_send, s_recv,
):
    me, rep = lax.axis_index("fsdp"), lax.axis_index("rep")
    tokens, depth = x.shape
    own_rows, width = w.shape
    slabs, bands, _ = bh.shape
    groups = mom.shape[0]
    scaling = 1.0 / math.sqrt(depth)
    bits = n.bit_length() - 1

    def peer(k):
        return sum((((me // 2**b) % 2 + (k >> b) % 2) % 2) * 2**b for b in range(bits))

    def across(d):
        return lax.rem(rep + d, reps)

    def columns(which):
        return pl.ds(pl.multiple_of(which * own_rows, LANES), own_rows)

    def to_peer(k, src, dst, send, recv):
        return pltpu.make_async_remote_copy(
            src_ref=src, dst_ref=dst, send_sem=send, recv_sem=recv,
            device_id={"fsdp": peer(k)}, device_id_type=pl.DeviceIdType.MESH,
        )

    def to_rep(d, src, dst, send, recv):
        return pltpu.make_async_remote_copy(
            src_ref=src, dst_ref=dst, send_sem=send, recv_sem=recv,
            device_id={"rep": across(d)}, device_id_type=pl.DeviceIdType.MESH,
        )

    loads = [
        pltpu.make_async_copy(x_hbm.at[0], x, load_sem.at[0]),
        pltpu.make_async_copy(og_hbm.at[0], og.at[0], load_sem.at[1]),
        pltpu.make_async_copy(w_hbm, w, load_sem.at[2]),
        pltpu.make_async_copy(mom_hbm.at[0], mom, load_sem.at[3]),
        pltpu.make_async_copy(x_hbm.at[0, :, columns(me)], oc.at[0], load_sem.at[4]),
    ]
    for load in loads:
        load.start()

    barrier = pltpu.get_barrier_semaphore()
    for d in range(1, reps):
        pl.semaphore_signal(
            barrier, inc=1, device_id={"rep": across(d)}, device_id_type=pl.DeviceIdType.MESH
        )
    for k in range(n - 1, 0, -1):
        pl.semaphore_signal(
            barrier, inc=1, device_id={"fsdp": peer(k)}, device_id_type=pl.DeviceIdType.MESH
        )
    pl.semaphore_wait(barrier, n - 1 + reps - 1)

    def crossings(k):
        return bin(k >> 1).count("1")

    relayed = [k for k in range(2, n, 2) if crossings(k) == 2]
    direct = [k for k in range(2, n, 2) if k not in relayed]
    order = sorted(range(2, n), key=lambda k: (-crossings(k), 1 - k % 2, k))
    og_copies = {
        k: to_peer(k, og_hbm.at[0], og.at[k], og_send.at[k], og_recv.at[k]) for k in direct + [1]
    }
    oc_copies = {
        k: to_peer(k, x_hbm.at[0, :, columns(peer(k))], oc.at[k], oc_send.at[k], oc_recv.at[k])
        for k in range(1, n)
    }
    forward = {
        k: to_peer(1, og.at[k], og.at[k + 1], og_send.at[k + 1], og_recv.at[k + 1])
        for k in range(2, n, 2)
    }
    relays = {}
    for k in relayed:
        low = k & -k
        for side, via in enumerate((low, k - low)):
            part = pl.ds(side * (tokens // 2), tokens // 2)
            relays[k, side] = to_peer(
                via, og.at[k - via, part], og.at[k, part], r_send.at[k, side], r_recv.at[k, side]
            )
    for copy in og_copies.values():
        copy.start()
    early = [k for k in order if crossings(k) > 1] + [1]
    for k in early:
        oc_copies[k].start()

    fill_basis(band_ref, bh, bl, bt)

    for k in direct:
        og_copies[k].wait_recv()
    for copy in relays.values():
        copy.start()
    for k in order:
        if k not in early:
            oc_copies[k].start()
    for k in direct:
        forward[k].start()

    loads[0].wait()
    span = slabs * LANES
    row = lax.broadcasted_iota(jnp.int32, (span, LANES), 0)
    lane = lax.broadcasted_iota(jnp.int32, (span, LANES), 1)
    for a in range(slabs):
        perm[:, a * LANES : (a + 1) * LANES] = (row == slabs * lane + a).astype(F32).astype(BF16)
    for piece in range(depth // span):
        sorted_piece = dot(x[:, piece * span : (piece + 1) * span], perm[...]).astype(BF16)
        for a in range(slabs):
            xa[a * tokens : (a + 1) * tokens, piece * LANES : (piece + 1) * LANES] = sorted_piece[
                :, a * LANES : (a + 1) * LANES
            ]
    for k in relayed:
        relays[k, 0].wait_recv()
        relays[k, 1].wait_recv()
        forward[k].start()

    for load in loads[1:]:
        load.wait()
    tiles = range(width // LANES)
    first = dot(oc[0], og[0], ((0,), (0,)))
    for t in tiles:
        grad[t] = first[:, t * LANES : (t + 1) * LANES]
    even[0] = dot(oc[0], w[...])
    to_partner = {}
    for k in [1] + order:
        oc_copies[k].wait_recv()
        if k % 2 and k > 1:
            forward[k - 1].wait_recv()
        elif k == 1:
            og_copies[1].wait_recv()
        product = dot(oc[k], og[k], ((0,), (0,)))
        for t in tiles:
            grad[t] += product[:, t * LANES : (t + 1) * LANES]
        partial = dot(oc[k], w[...])
        if k % 2:
            odd[k // 2] = partial.astype(BF16)
            to_partner[k] = to_peer(1, odd.at[k // 2], pin.at[k // 2], p_send.at[k // 2], p_recv.at[k // 2])
            to_partner[k].start()
        else:
            even[k // 2] = partial

    v_copies = {}
    for h in range(n // 2 - 1, 0, -1):
        to_partner[2 * h + 1].wait_recv()
        pout[h] = (even[h] + pin[h].astype(F32)).astype(BF16)
        copy = to_peer(2 * h, pout.at[h], vin.at[h], v_send.at[h], v_recv.at[h])
        copy.start()
        v_copies[h] = copy

    wide, narrow = None, None
    for a in range(slabs):
        rows = [grad[t, pl.ds(a, groups, stride=slabs), :] for t in tiles]
        part = MOMENTUM_DECAY * mom[:, a * width : (a + 1) * width] + scaling * jnp.concatenate(rows, 1)
        mom[:, a * width : (a + 1) * width] = part
        hi, lo = split_hi_lo(part)
        both = dot(hi, bt[a * width : (a + 1) * width, :])
        rest = dot(lo, bt[a * width : (a + 1) * width, :bands])
        wide = both if wide is None else wide + both
        narrow = rest if narrow is None else narrow + rest
    total = wide[:, :bands] + (wide[:, bands:] + narrow)
    cz[rep] = total.astype(BF16)
    c_copies = [to_rep(d, cz.at[rep], cz.at[rep], c_send.at[d], c_recv.at[d]) for d in range(1, reps)]
    for c in c_copies:
        c.start()

    c_hi, c_lo = split_hi_lo(total)
    for a in range(slabs):
        cut = slice(a * width, (a + 1) * width)
        left[0, :, cut] = mom[:, cut] - dot3(c_hi, c_lo, bh[a], bl[a])

    for c in c_copies:
        c.wait_recv()
    shared = cz[0].astype(F32)
    for d in range(1, reps):
        shared = shared + cz[d].astype(F32)
    shared = shared / reps
    sg[me] = shared.astype(BF16)
    s_copies = [to_peer(k, sg.at[me], sg.at[me], s_send.at[k], s_recv.at[k]) for k in range(n - 1, 0, -1)]
    for s in s_copies:
        s.start()

    s_hi, s_lo = split_hi_lo(shared)
    for a in range(slabs):
        product = dot3(s_hi, s_lo, bh[a], bl[a])
        for t in tiles:
            upd[t, pl.ds(a, groups, stride=slabs), :] = product[:, t * LANES : (t + 1) * LANES]
    for t in tiles:
        cut = slice(t * LANES, (t + 1) * LANES)
        nw[:, cut] = rebuild_rows(w[:, cut], upd[t])

    to_partner[1].wait_recv()
    base = even[0] + pin[0].astype(F32)
    for h in range(1, n // 2):
        v_copies[h].wait_recv()
        base = base + vin[h].astype(F32)
    for s in s_copies:
        s.wait_recv()
    mixed = dot(xa[...], sg[...].reshape(n * groups, bands))
    mixed = jnp.concatenate([mixed[a * tokens : (a + 1) * tokens] for a in range(slabs)], 1)
    hi, lo = split_hi_lo(mixed)
    change = dot3(hi, lo, bh[...].reshape(slabs * bands, width), bl[...].reshape(slabs * bands, width))
    val[0] = ((base - LEARNING_RATE * change) * scaling).astype(BF16)

    for k in range(1, n):
        oc_copies[k].wait_send()
        if k % 2 and k > 1:
            forward[k - 1].wait_send()
        elif k in relayed:
            relays[k, 0].wait_send()
            relays[k, 1].wait_send()
        else:
            og_copies[k].wait_send()
        if k % 2:
            to_partner[k].wait_send()
    for copy in list(v_copies.values()) + c_copies + s_copies:
        copy.wait_send()


def store_kernel(left, nw, val, left_hbm, nw_hbm, val_hbm, sems):
    copies = [
        pltpu.make_async_copy(src, dst, sems.at[i])
        for i, (src, dst) in enumerate(((left, left_hbm), (nw, nw_hbm), (val, val_hbm)))
    ]
    for copy in copies:
        copy.start()
    for copy in copies:
        copy.wait()


def fused_shards(n, reps, inputs, out_grad, weight, momentum, band_index):
    tokens, depth = inputs.shape[1:]
    own_rows, width = weight.shape
    groups, group_len = momentum.shape[1:]
    slabs, bands = group_len // width, band_index.shape[0]
    half = n // 2
    dma = pltpu.SemaphoreType.DMA
    span = slabs * LANES
    anywhere = pl.BlockSpec(memory_space=pl.ANY)
    held = pl.pallas_call(
        functools.partial(kernel, n, reps),
        out_shape=(
            pltpu.VMEM(momentum.shape, F32),
            pltpu.VMEM(weight.shape, BF16),
            pltpu.VMEM(out_grad.shape, BF16),
        ),
        in_specs=[pl.BlockSpec(memory_space=pltpu.VMEM)] + [anywhere] * 4,
        out_specs=(pl.BlockSpec(memory_space=pltpu.VMEM),) * 3,
        scratch_shapes=[
            pltpu.VMEM((tokens, depth), BF16),
            pltpu.VMEM((n, tokens, own_rows), BF16),
            pltpu.VMEM((n, tokens, width), BF16),
            pltpu.VMEM((own_rows, width), BF16),
            pltpu.VMEM((groups, group_len), F32),
            pltpu.VMEM((slabs, bands, width), BF16),
            pltpu.VMEM((slabs, bands, width), BF16),
            pltpu.VMEM((group_len, 2 * bands), BF16),
            pltpu.VMEM((span, span), BF16),
            pltpu.VMEM((slabs * tokens, depth // slabs), BF16),
            pltpu.VMEM((width // LANES, own_rows, LANES), F32),
            pltpu.VMEM((width // LANES, own_rows, LANES), F32),
            pltpu.VMEM((half, tokens, width), BF16),
            pltpu.VMEM((half, tokens, width), F32),
            pltpu.VMEM((half, tokens, width), BF16),
            pltpu.VMEM((half, tokens, width), BF16),
            pltpu.VMEM((half, tokens, width), BF16),
            pltpu.VMEM((reps, groups, bands), BF16),
            pltpu.VMEM((n, groups, bands), BF16),
            dma((5,)),
            dma((n,)), dma((n,)), dma((n,)), dma((n,)), dma((n, 2)), dma((n, 2)),
            dma((half,)), dma((half,)), dma((half,)), dma((half,)),
            dma((reps,)), dma((reps,)), dma((n,)), dma((n,)),
        ],
        compiler_params=pltpu.CompilerParams(collective_id=0, has_side_effects=True),
    )(band_index.reshape(1, -1), inputs, out_grad, weight, momentum)
    return pl.pallas_call(
        store_kernel,
        out_shape=tuple(jax.ShapeDtypeStruct(a.shape, a.dtype) for a in held),
        in_specs=[anywhere] * 3,
        out_specs=(anywhere,) * 3,
        scratch_shapes=[dma((3,))],
        compiler_params=pltpu.CompilerParams(vmem_limit_bytes=1 << 20),
    )(*held)


def fits_kernel(n, inputs, weight, momentum, band_index):
    tokens, depth = inputs.shape[1:]
    own_rows, width = weight.shape
    groups, group_len = momentum.shape[1:]
    return (
        n > 1
        and n & (n - 1) == 0
        and group_len & (group_len - 1) == 0
        and tokens % 32 == 0
        and own_rows % LANES == 0
        and width % LANES == 0
        and groups % 16 == 0
        and group_len % width == 0
        and group_len // LANES <= LANES
        and depth % (group_len // width * LANES) == 0
        and band_index.shape[0] % LANES == 0
    )


def program(n, reps, inputs, out_grad, weight, momentum, band_index):
    if fits_kernel(n, inputs, weight, momentum, band_index):
        return fused_shards(n, reps, inputs, out_grad, weight, momentum, band_index)
    return shards(inputs, out_grad, weight, momentum, band_index)


def solution(mesh):
    placed = (
        P("rep", "fsdp", None),
        P("rep", "fsdp", None),
        P("fsdp", None),
        P("rep", "fsdp", None),
        P(),
    )
    return jax.shard_map(
        functools.partial(program, mesh.shape["fsdp"], mesh.shape["rep"]),
        mesh=mesh,
        in_specs=placed,
        out_specs=(P("rep", "fsdp", None), P("fsdp", None), P("rep", "fsdp", None)),
        check_vma=False,
    )
```
